256 devices in a mesh: ctx: 8 (over x, y_hi), mp: 32 (over y_lo, z, core).
Axes of the slice: x: 4, y: 4 (y_hi: 2, y_lo: 2; y = y_hi * 2 + y_lo), z: 8, core: 2. Of those that a mesh axis runs over, the one named last changes fastest.
Arguments:
- hidden_states: bfloat16 [24576, 8192], P('ctx', 'mp'), may hold values from -8 to 8
- route_slot: int32 [4608], P('ctx'), may hold values from 0 to 3071, as said below
- route_live: int32 [4608], P('ctx'), may hold values from 0 to 1, as said below
- router_weight: bfloat16 [8192], replicated, may hold values from -0.0625 to 0.0625
- query_weight: bfloat16 [8192, 8192], P(None, 'mp')
- keyval_weight: bfloat16 [8192, 2048], P(None, 'mp')
- output_weight: bfloat16 [8192, 8192], P('mp'), may hold values from -0.75 to 0.75
Outputs:
- mixed_states: bfloat16 [24576, 8192], P('ctx', 'mp')
The draws below stay inside these ranges and needn't reach their ends.
Inputs may be any that keep to these rules, and one draw needn't show every extreme that they name: `route_slot`: within each owner's 576 slots the live slots come first and hold distinct ascending offsets below 3072; dead slots hold 0. The last token of every owner is routed. `route_live`: each owner has from 192 to 576 live slots, all at its first slots; together they are exactly 3072; some owner has all 576 live.
All inputs are finite; a program needn't handle non-finite values.
Results may differ from the reference program's by a relative error of at most 0.03.
Values may be sent and summed in bfloat16 or wider, within the bound.
No kernel may reach another device: no remote copies, remote signals or barrier semaphores. Data moves between devices by JAX's collectives and lax.ppermute only.
A program may use at most 128 MiB of HBM per device.

```python
import jax
import jax.numpy as jnp
from jax import lax

MODEL_WIDTH = 8192
HEAD_SIZE = 128
GROUP = 8
HQ_DEV = 2
HQ = 64
KEYVAL_HEADS = 8
SEQ_DEV = 3072
LENGTH = 24576
RQ = 384
SLOTS = 576
ROUTED = 3072
N_CTX = 8


def draw_hidden_states(key, part):
    drawn = jax.random.normal(key, (LENGTH, MODEL_WIDTH), jnp.float32)
    return jnp.clip(drawn, -8.0, 8.0).astype(jnp.bfloat16)


def keyval_lookup_table(key):
    unscaled_scores = jax.random.normal(jax.random.fold_in(key, 11), (MODEL_WIDTH, KEYVAL_HEADS * 2 * HEAD_SIZE), jnp.float32)
    return jnp.clip(unscaled_scores, -6.0, 6.0) * MODEL_WIDTH ** (-0.5)


def draw_keyval_weight(key, part):
    return keyval_lookup_table(key).astype(jnp.bfloat16)


def draw_query_weight(key, part):
    unscaled_scores = jax.random.normal(jax.random.fold_in(key, 13), (MODEL_WIDTH, HQ * HEAD_SIZE), jnp.float32)
    fresh = jnp.clip(unscaled_scores, -6.0, 6.0) * (2.0 * MODEL_WIDTH ** (-0.5))
    return fresh.astype(jnp.bfloat16)


def route_table(key):
    base_key = jax.random.fold_in(key, 5)
    order_key, spread_key, pick_key = jax.random.split(base_key, 3)
    shuffled = jax.random.permutation(order_key, N_CTX)
    spread_amount = jax.random.randint(spread_key, (N_CTX // 2,), 0, RQ // 2 + 1)
    spread_amount = spread_amount.at[0].set(RQ // 2)
    paired = jnp.stack([RQ + spread_amount, RQ - spread_amount], axis=1).reshape(N_CTX).astype(jnp.int32)
    counts = jnp.zeros((N_CTX,), jnp.int32).at[shuffled].set(paired)
    pick_keys = jax.random.split(pick_key, N_CTX)

    def one_owner(owner_key, amount):
        ordering = jax.random.permutation(owner_key, SEQ_DEV - 1)
        chosen = jnp.concatenate([(ordering < amount - 1).astype(jnp.int32), jnp.ones((1,), jnp.int32)])
        sorted_slots = jnp.argsort(1 - chosen, stable=True)[:SLOTS].astype(jnp.int32)
        live_flags = (jnp.arange(SLOTS) < amount).astype(jnp.int32)
        return (sorted_slots * live_flags, live_flags)
    slot_table, live_table = jax.vmap(one_owner)(pick_keys, counts)
    return (slot_table.reshape(N_CTX * SLOTS).astype(jnp.int32), live_table.reshape(N_CTX * SLOTS).astype(jnp.int32))


def draw_route_slot(key, part):
    return route_table(key)[0]


def draw_route_live(key, part):
    return route_table(key)[1]


def spiked(array, rng, source, target, blocks, factor):
    owner, partner = [(jnp.arange(array.shape[dim]) // (array.shape[dim] // blocks)).reshape([-1 if axis == dim else 1 for axis in range(array.ndim)]) for dim in (source, target)]
    chosen = jax.random.permutation(rng, blocks)[partner]
    strong = (owner == chosen) | (owner == (partner + blocks // 2) % blocks)
    return jnp.where(strong, factor * array, array)


def levels(key, extent, shards, low, top_value):
    level, own = 1.0, jax.random.fold_in(key, 6)
    for axis_at, parts in shards:
        draws = jnp.exp(jax.random.uniform(jax.random.fold_in(own, axis_at), (parts,), jnp.float32, low / len(shards), top_value / len(shards)))
        level = level * jnp.repeat(draws, extent[axis_at] // parts).reshape([-1 if axis == axis_at else 1 for axis in range(len(extent))])
    return level


def gaussian(key, extent, deviation, reach, cuts=(), held_as=jnp.bfloat16):
    loudness = levels(key, extent, cuts, -0.22, 0.18) if cuts else 1.0
    entries = jax.random.normal(key, extent, jnp.float32) * deviation * loudness
    return jnp.minimum(jnp.maximum(entries, -reach), reach).astype(held_as)


def bell_draw_with(rng, dims, spread, reach, cuts, heavy, kind=jnp.bfloat16):
    array = spread * jax.random.normal(rng, dims, jnp.float32)
    if cuts:
        array = array * levels(rng, dims, cuts, -0.22, 0.18)
    return jnp.clip(spiked(array, jax.random.fold_in(rng, 3), *heavy), -reach, reach).astype(kind)


def setup_inputs(seed: int = 0) -> dict:
    keys = jax.random.split(jax.random.key(seed), 8)
    hidden_states = draw_hidden_states(jax.random.fold_in(keys[7], 71), 0)
    route_slot = draw_route_slot(jax.random.fold_in(keys[7], 71), 0)
    route_live = draw_route_live(jax.random.fold_in(keys[7], 71), 0)
    router_weight = gaussian(keys[3], (MODEL_WIDTH,), MODEL_WIDTH ** -0.5, 0.0625)
    query_weight = draw_query_weight(jax.random.fold_in(keys[7], 71), 0)
    keyval_weight = draw_keyval_weight(jax.random.fold_in(keys[7], 71), 0)
    output_weight = bell_draw_with(keys[6], (HQ * HEAD_SIZE, MODEL_WIDTH), (HQ_DEV * HEAD_SIZE) ** -0.5, 0.75, ((0, 32),), (0, 1, 32, 2.75))
    return {"hidden_states": hidden_states, "route_slot": route_slot, "route_live": route_live, "router_weight": router_weight, "query_weight": query_weight, "keyval_weight": keyval_weight, "output_weight": output_weight}


def reference(hidden_states, route_slot, route_live, router_weight, query_weight, keyval_weight, output_weight):
    live_mask = route_live.reshape(N_CTX, SLOTS)
    counts = jnp.sum(live_mask, axis=1).astype(jnp.int32)
    run_ends = jnp.cumsum(counts).astype(jnp.int32)
    run_starts = run_ends - counts
    rank_ids = jnp.arange(ROUTED, dtype=jnp.int32)
    owners = jnp.sum((run_ends[None, :] <= rank_ids[:, None]).astype(jnp.int32), axis=1).astype(jnp.int32)
    first_rank = jnp.take(run_starts, owners).astype(jnp.int32)
    slot_index = (owners * SLOTS + rank_ids - first_rank).astype(jnp.int32)
    positions = (owners * SEQ_DEV + jnp.take(route_slot, slot_index)).astype(jnp.int32)
    routed = jnp.take(hidden_states, positions, axis=0)
    gate_value = jax.nn.sigmoid(jnp.dot(routed, router_weight, preferred_element_type=jnp.float32))
    queries = jnp.dot(routed, query_weight, preferred_element_type=jnp.float32).astype(jnp.bfloat16)
    keyvals = jnp.dot(routed, keyval_weight, preferred_element_type=jnp.float32).astype(jnp.bfloat16)
    allowed = rank_ids[None, :] <= rank_ids[:, None]

    def one_head(head_index):
        head_query = lax.dynamic_slice_in_dim(queries, head_index * HEAD_SIZE, HEAD_SIZE, 1)
        kv_start = (head_index // GROUP) * 2 * HEAD_SIZE
        head_keys = lax.dynamic_slice_in_dim(keyvals, kv_start, HEAD_SIZE, 1)
        head_values = lax.dynamic_slice_in_dim(keyvals, kv_start + HEAD_SIZE, HEAD_SIZE, 1)
        scores = jnp.dot(head_query, head_keys.T, preferred_element_type=jnp.float32) * (HEAD_SIZE ** -0.5)
        masked = jnp.where(allowed, scores, -1e30)
        row_max = jnp.max(masked, axis=1, keepdims=True)
        weights = jnp.where(allowed, jnp.exp(masked - row_max), 0.0)
        row_sum = jnp.sum(weights, axis=1, keepdims=True)
        return (jnp.dot(weights.astype(jnp.bfloat16), head_values, preferred_element_type=jnp.float32) / row_sum).astype(jnp.bfloat16)

    def group_step(combined, group_index):
        pieces = [one_head(group_index * HQ_DEV + inner) for inner in range(HQ_DEV)]
        attended = jnp.concatenate(pieces, axis=1)
        out_rows = lax.dynamic_slice_in_dim(output_weight, group_index * HQ_DEV * HEAD_SIZE, HQ_DEV * HEAD_SIZE, 0)
        head_part = jnp.dot(attended, out_rows, preferred_element_type=jnp.float32).astype(jnp.bfloat16)
        head_part = lax.optimization_barrier(head_part)
        return combined + head_part.astype(jnp.float32), None

    combined, unused = lax.scan(group_step, jnp.zeros((ROUTED, MODEL_WIDTH), jnp.float32), jnp.arange(HQ // HQ_DEV, dtype=jnp.int32))
    update = (gate_value[:, None] * combined).astype(jnp.bfloat16)
    widened = hidden_states.astype(jnp.float32).at[positions].add(update.astype(jnp.float32))
    return widened.astype(jnp.bfloat16)
```

```python
import functools

import jax
import jax.numpy as jnp
from jax import lax
from jax.experimental import pallas as pl
from jax.experimental.pallas import tpu as pltpu
from jax.sharding import PartitionSpec as P

BF = jnp.bfloat16
F32 = jnp.float32
CTX = 8
NY, NZ, NC = 2, 8, 2
HEAD = 128
WIDTH = 256
FAR = 1 << 29
VMEM_LIMIT = 50 * 1024 * 1024


def mp_perm(move):
    pairs = []
    for i in range(NY * NZ * NC):
        y, z, c = i // (NZ * NC), (i // NC) % NZ, i % NC
        y, z, c = move(y, z, c)
        pairs.append((i, (y * NZ + z) * NC + c))
    return pairs


UP = mp_perm(lambda y, z, c: (y, (z + 1) % NZ, c))
DOWN = mp_perm(lambda y, z, c: (y, (z - 1) % NZ, c))
ACROSS = mp_perm(lambda y, z, c: (1 - y, z, c))
SIBLING = mp_perm(lambda y, z, c: (y, z, 1 - c))
PARTNER = mp_perm(lambda y, z, c: (y, z ^ 1, c))


def send(value, pairs):
    return lax.ppermute(value, "mp", pairs)


def params(**more):
    return pltpu.CompilerParams(vmem_limit_bytes=VMEM_LIMIT, **more)


def gather_kernel(slot_ref, hidden_ref, first_ref, second_ref):
    rows = slot_ref.shape[1]
    tokens = hidden_ref.shape[0]
    spread = jnp.transpose(jnp.broadcast_to(slot_ref[...], (128, rows)))
    lane = lax.broadcasted_iota(jnp.int32, (rows, 128), 1)
    total = jnp.zeros((rows, WIDTH), F32)
    for step in range(tokens // 256):
        parts = [
            (spread == lane + (step * 256 + part * 128)).astype(F32).astype(BF) for part in range(2)
        ]
        total += jnp.dot(
            jnp.concatenate(parts, axis=1),
            hidden_ref[step * 256 : (step + 1) * 256, :],
            preferred_element_type=F32,
        )
    cut = first_ref.shape[0]
    first_ref[...] = total[:cut].astype(BF)
    second_ref[...] = total[cut:].astype(BF)


def gather_rows(hidden, slot, cut):
    rows = slot.shape[0]
    return pl.pallas_call(
        gather_kernel,
        out_shape=(
            jax.ShapeDtypeStruct((cut, WIDTH), BF),
            jax.ShapeDtypeStruct((rows - cut, WIDTH), BF),
        ),
        compiler_params=params(),
        cost_estimate=pl.CostEstimate(
            flops=2 * rows * hidden.shape[0] * WIDTH, bytes_accessed=2_500_000, transcendentals=0
        ),
    )(slot.reshape(1, rows), hidden)


def scatter_kernel(slot_ref, gate_ref, first_ref, second_ref, hidden_ref, out_ref):
    rows = slot_ref.shape[1]
    combined = jnp.concatenate([first_ref[...], second_ref[...]], axis=0)
    update = (jax.nn.sigmoid(gate_ref[:, 0:1]) * combined).astype(BF)
    tile = hidden_ref.shape[0]
    token = lax.broadcasted_iota(jnp.int32, (tile, rows), 0) + pl.program_id(0) * tile
    chosen = (token == slot_ref[...]).astype(F32).astype(BF)
    addition = jnp.dot(chosen, update, preferred_element_type=F32)
    out_ref[...] = (hidden_ref[...].astype(F32) + addition).astype(BF)


def scatter_rows(hidden, slot, logit, first, second):
    tokens = hidden.shape[0]
    rows = slot.shape[0]
    tile = 512
    whole = lambda shape: pl.BlockSpec(shape, lambda i: (0, 0))
    return pl.pallas_call(
        scatter_kernel,
        grid=(tokens // tile,),
        in_specs=[
            whole((1, rows)),
            whole(logit.shape),
            whole(first.shape),
            whole(second.shape),
            pl.BlockSpec((tile, WIDTH), lambda i: (i, 0)),
        ],
        out_specs=pl.BlockSpec((tile, WIDTH), lambda i: (i, 0)),
        out_shape=jax.ShapeDtypeStruct((tokens, WIDTH), BF),
        compiler_params=params(),
        cost_estimate=pl.CostEstimate(
            flops=2 * rows * tokens * WIDTH, bytes_accessed=4_000_000, transcendentals=0
        ),
    )(slot.reshape(1, rows), logit, first, second, hidden)


def halves_kernel(place_ref, query_ref, keyval_ref, output_ref, q_ref, kv_ref, o_ref):
    q_ref[...] = query_ref[...]
    kv_ref[...] = keyval_ref[...]
    o_ref[...] = output_ref[...]


def sibling_halves(place, query_weight, keyval_t, output_weight):
    count = NY * NZ
    return pl.pallas_call(
        halves_kernel,
        grid_spec=pltpu.PrefetchScalarGridSpec(
            num_scalar_prefetch=1,
            grid=(count,),
            in_specs=[
                pl.BlockSpec((WIDTH, WIDTH), lambda i, p: (2 * i + 1 - p[2], 0)),
                pl.BlockSpec((64, WIDTH), lambda i, p: (0, 2 * i + 1 - p[2])),
                pl.BlockSpec((WIDTH, WIDTH), lambda i, p: (0, 2 * i + 1 - p[2])),
            ],
            out_specs=[
                pl.BlockSpec((WIDTH, WIDTH), lambda i, p: (i, 0)),
                pl.BlockSpec((64, WIDTH), lambda i, p: (0, i)),
                pl.BlockSpec((WIDTH, WIDTH), lambda i, p: (0, i)),
            ],
        ),
        out_shape=(
            jax.ShapeDtypeStruct((count * WIDTH, WIDTH), BF),
            jax.ShapeDtypeStruct((64, count * WIDTH), BF),
            jax.ShapeDtypeStruct((WIDTH, count * WIDTH), BF),
        ),
        compiler_params=params(),
        cost_estimate=pl.CostEstimate(flops=0, bytes_accessed=9_000_000, transcendentals=0),
    )(place, query_weight, keyval_t, output_weight)


def project_weight_kernel(
    place_ref, q0, q1, sq0, sq1, kv0, kv1, skv0, skv1, r0, r1, out_ref
):
    core = place_ref[2]
    for part, (own_q, sib_q, own_kv, sib_kv, router) in enumerate(
        ((q0, sq0, kv0, skv0, r0), (q1, sq1, kv1, skv1, r1))
    ):
        rows = slice(part * WIDTH, (part + 1) * WIDTH)
        out_ref[0, rows, 0:256] = own_q[...]
        out_ref[0, rows, 256:512] = sib_q[...]
        mine, theirs = own_kv[...].astype(F32), sib_kv[...].astype(F32)
        low = jnp.where(core == 0, mine, theirs)
        high = jnp.where(core == 0, theirs, mine)
        out_ref[0, rows, 512:640] = jnp.transpose(jnp.concatenate([low, high], axis=0)).astype(BF)
        spread = jnp.broadcast_to(router[0].astype(F32), (128, WIDTH))
        out_ref[0, rows, 640:768] = jnp.transpose(spread).astype(BF)


def project_weights(place, query_weight, sib_query, keyval_t, sib_keyval_t, router_weight):
    def both(shape, index):
        return [
            pl.BlockSpec(shape, functools.partial(index, 0)),
            pl.BlockSpec(shape, functools.partial(index, 1)),
        ]

    def spot(part, i, p):
        y = jnp.where(part == 0, p[0], 1 - p[0])
        return y * NZ + lax.rem(p[1] + i, NZ)

    specs = (
        both((WIDTH, WIDTH), lambda part, i, p: (2 * spot(part, i, p) + p[2], 0))
        + both((WIDTH, WIDTH), lambda part, i, p: (spot(part, i, p), 0))
        + both((64, WIDTH), lambda part, i, p: (0, 2 * spot(part, i, p) + p[2]))
        + both((64, WIDTH), lambda part, i, p: (0, spot(part, i, p)))
        + both((1, 1, WIDTH), lambda part, i, p: (2 * spot(part, i, p) + p[2], 0, 0))
    )
    router = router_weight.reshape(NY * NZ * NC, 1, WIDTH)
    return pl.pallas_call(
        project_weight_kernel,
        grid_spec=pltpu.PrefetchScalarGridSpec(
            num_scalar_prefetch=1,
            grid=(NZ,),
            in_specs=specs,
            out_specs=pl.BlockSpec((1, 512, 768), lambda i, p: (i, 0, 0)),
        ),
        out_shape=jax.ShapeDtypeStruct((NZ, 512, 768), BF),
        compiler_params=params(),
        cost_estimate=pl.CostEstimate(flops=0, bytes_accessed=12_000_000, transcendentals=0),
    )(
        place, query_weight, query_weight, sib_query, sib_query, keyval_t, keyval_t,
        sib_keyval_t, sib_keyval_t, router, router,
    )


def output_weight_kernel(place_ref, o0, o1, so0, so1, out_ref):
    out_ref[0, 0:256, 0:256] = o0[...]
    out_ref[0, 0:256, 256:512] = o1[...]
    out_ref[0, 256:512, 0:256] = so0[...]
    out_ref[0, 256:512, 256:512] = so1[...]


def output_weights(place, output_weight, sib_output):
    def spot(part, i, p):
        y = p[0] if part == 0 else 1 - p[0]
        return y * NZ + lax.rem(p[1] + i, NZ)

    block = (WIDTH, WIDTH)
    return pl.pallas_call(
        output_weight_kernel,
        grid_spec=pltpu.PrefetchScalarGridSpec(
            num_scalar_prefetch=1,
            grid=(NZ,),
            in_specs=[
                pl.BlockSpec(block, lambda i, p: (0, 2 * spot(0, i, p) + p[2])),
                pl.BlockSpec(block, lambda i, p: (0, 2 * spot(1, i, p) + p[2])),
                pl.BlockSpec(block, lambda i, p: (0, spot(0, i, p))),
                pl.BlockSpec(block, lambda i, p: (0, spot(1, i, p))),
            ],
            out_specs=pl.BlockSpec((1, 512, 512), lambda i, p: (i, 0, 0)),
        ),
        out_shape=jax.ShapeDtypeStruct((NZ, 512, 512), BF),
        compiler_params=params(),
        cost_estimate=pl.CostEstimate(flops=0, bytes_accessed=8_000_000, transcendentals=0),
    )(place, output_weight, output_weight, sib_output, sib_output)


def attend_kernel(rank_ref, query_ref, *refs):
    pieces = (len(refs) - 1) // 2
    keyvals, key_ranks, out_ref = refs[:pieces], refs[pieces : 2 * pieces], refs[-1]
    scale = HEAD ** (-0.5)
    own_rank = rank_ref[:, 0:1]
    masked = []
    for keyval, key_rank in zip(keyvals, key_ranks):
        scores = lax.dot_general(
            query_ref[...],
            keyval[:, 0:HEAD],
            (((1,), (1,)), ((), ())),
            preferred_element_type=F32,
        )
        masked.append(jnp.where(key_rank[...] <= own_rank, scores * scale, -1e30))
    top = functools.reduce(
        jnp.maximum, [jnp.max(part, axis=1, keepdims=True) for part in masked]
    )
    total = jnp.zeros_like(top)
    result = jnp.zeros((query_ref.shape[0], HEAD), F32)
    for keyval, part in zip(keyvals, masked):
        weights = jnp.exp(part - top)
        total += jnp.sum(weights, axis=1, keepdims=True)
        result += jnp.dot(weights.astype(BF), keyval[:, HEAD:], preferred_element_type=F32)
    out_ref[...] = (result / total).astype(BF)


def attend(query_rank, queries, keyvals, key_ranks, tile):
    rows = queries.shape[0]
    keys = sum(piece.shape[0] for piece in keyvals)
    whole = lambda piece: pl.BlockSpec(piece.shape, lambda i, h: (0, 0))
    return pl.pallas_call(
        attend_kernel,
        grid=(rows // tile, queries.shape[1] // HEAD),
        in_specs=[
            pl.BlockSpec((tile, 128), lambda i, h: (i, 0)),
            pl.BlockSpec((tile, HEAD), lambda i, h: (i, h)),
            *[whole(piece) for piece in keyvals],
            *[whole(piece) for piece in key_ranks],
        ],
        out_specs=pl.BlockSpec((tile, HEAD), lambda i, h: (i, h)),
        out_shape=jax.ShapeDtypeStruct(queries.shape, BF),
        compiler_params=params(),
        cost_estimate=pl.CostEstimate(
            flops=8 * rows * keys * HEAD, bytes_accessed=4_000_000, transcendentals=2 * rows * keys
        ),
    )(query_rank, queries, *keyvals, *key_ranks)


def ring(value):
    half = value.shape[0] // 2
    found = {0: value}
    up = down = value
    for step in (1, 2, 3):
        up, down = send(up, UP), send(down, DOWN)
        found[NZ - step], found[step] = up, down
    found[4] = jnp.concatenate([send(up[:half], UP), send(down[half:], DOWN)], axis=0)
    return found


def ring_sum(term, rows):
    half = rows // 2
    last = term(4)
    up = send(last[:half].astype(BF), UP).astype(F32)
    down = send(last[half:].astype(BF), DOWN).astype(F32)
    third, fifth = term(3), term(5)
    up = jnp.concatenate([third[:half] + up, third[half:]], axis=0)
    down = jnp.concatenate([fifth[:half], fifth[half:] + down], axis=0)
    for step in (2, 1, 0):
        up = send(up.astype(BF), UP).astype(F32)
        down = send(down.astype(BF), DOWN).astype(F32)
        if step:
            up, down = up + term(step), down + term(NZ - step)
    return term(0) + up + down


def own_half(value, core):
    half = value.shape[0] // 2
    return lax.dynamic_slice_in_dim(value, core * half, half, 0)


def local(
    hidden_states, route_slot, route_live, router_weight, query_weight, keyval_weight, output_weight
):
    slots = route_slot.shape[0]
    cut = slots // 2
    ctx = lax.axis_index("ctx")
    mp = lax.axis_index("mp")
    y, z, core = mp // (NZ * NC), lax.rem(mp // NC, NZ), lax.rem(mp, NC)
    place = jnp.stack([y, z, core]).astype(jnp.int32)

    first, second = gather_rows(hidden_states, route_slot, cut)

    keyval_t = keyval_weight.T
    out_q, out_kv, out_o = sibling_halves(place, query_weight, keyval_t, output_weight)
    sib_q, sib_kv, sib_o = (send(part, SIBLING) for part in (out_q, out_kv, out_o))
    weights = project_weights(place, query_weight, sib_q, keyval_t, sib_kv, router_weight)
    out_weights = output_weights(place, output_weight, sib_o)

    count = jnp.sum(route_live).astype(jnp.int32)
    counts = lax.all_gather(count.reshape(1), "ctx", axis=0, tiled=True)
    owner_ids = jnp.arange(CTX)
    starts = jnp.sum(jnp.where(owner_ids[None, :] < owner_ids[:, None], counts[None, :], 0), axis=1)

    def ranks(owner, slot):
        return jnp.where(slot < counts[owner], starts[owner] + slot, 2 * FAR)

    def dot(rows, weight):
        return jnp.dot(rows, weight, preferred_element_type=F32)

    doubled = jnp.concatenate([first, send(first, ACROSS)], axis=1)
    found_first = ring(doubled)
    found_second = ring(second)
    crossed = {e: send(value, ACROSS) for e, value in found_second.items()}

    order = (0, 1, 7, 2, 6, 3, 5, 4)
    sum_first = sum(dot(found_first[e], weights[e]) for e in order)
    sum_second = sum(
        dot(found_second[e], weights[e, :WIDTH]) + dot(crossed[e], weights[e, WIDTH:]) for e in order
    )

    queries, logits, keyvals, key_ranks = [], [], [], []
    sources = lax.rem(ctx + CTX - jnp.arange(CTX), CTX)
    for base, partial in ((0, sum_first), (cut, sum_second)):
        rows = partial.shape[0]
        other = send(partial[:, WIDTH:], SIBLING)
        queries.append((partial[:, :WIDTH] + other[:, :WIDTH]).astype(BF))
        logits.append(partial[:, 640:768] + other[:, 384:512])
        mine = own_half((partial[:, 512:640] + other[:, 256:384]).astype(BF), core)
        theirs = send(mine, PARTNER)
        even = lax.rem(z, 2) == 0
        keyval = jnp.concatenate(
            [jnp.where(even, mine, theirs), jnp.where(even, theirs, mine)], axis=1
        )
        gathered = [keyval] + [
            lax.ppermute(keyval, "ctx", [(i, (i + d) % CTX) for i in range(CTX)])
            for d in range(1, CTX)
        ]
        piece = jnp.concatenate(gathered, axis=0)
        keyvals += [piece, send(piece, SIBLING)]
        row = jnp.arange(rows // 2)
        for part in (core, 1 - core):
            slot = base + part * (rows // 2) + row
            rank = ranks(sources[:, None], slot[None, :])
            key_ranks.append(rank.reshape(1, -1))

    slot_ids = jnp.arange(slots)
    own_rank = jnp.where(slot_ids < count, starts[ctx] + slot_ids, FAR)
    own_rank = jnp.broadcast_to(own_rank[:, None], (slots, 128))
    attended = attend(own_rank, jnp.concatenate(queries, axis=0), keyvals, key_ranks, 288)

    chip = jnp.concatenate([attended, send(attended, SIBLING)], axis=1)
    chip_first, chip_second = chip[:cut], chip[cut:]

    def term_first(e):
        return dot(chip_first, out_weights[e])

    def term_second(e):
        outgoing = dot(chip_second, out_weights[e, :, WIDTH:]).astype(BF)
        return dot(chip_second, out_weights[e, :, :WIDTH]) + send(outgoing, ACROSS).astype(F32)

    total_second = ring_sum(term_second, slots - cut)
    total_first = ring_sum(term_first, cut)
    total_first = total_first[:, :WIDTH] + send(total_first[:, WIDTH:].astype(BF), ACROSS).astype(F32)

    live_slot = jnp.where(route_live == 1, route_slot, -1)
    return scatter_rows(
        hidden_states, live_slot, jnp.concatenate(logits, axis=0), total_first, total_second
    )


def solution(mesh):
    placed = (P("ctx", "mp"), P("ctx"), P("ctx"), P(), P(None, "mp"), P(None, "mp"), P("mp", None))
    return jax.shard_map(
        local, mesh=mesh, in_specs=placed, out_specs=P("ctx", "mp"), check_vma=False
    )
```
